32 devices in a mesh: groups: 2 (over y), replica: 16 (over z, x, core).
Axes of the slice: x: 2, y: 2, z: 4, core: 2. Of those that a mesh axis runs over, the one named last changes fastest.
Arguments:
- queries: bfloat16 [64, 4, 4096], P(('groups', 'replica')), parts along dimension 0, may hold values from -4 to 4
- keys: bfloat16 [64, 4, 4096], P(('groups', 'replica')), parts along dimension 0, may hold values from -4 to 4
- values: bfloat16 [64, 4, 4096], P(('groups', 'replica')), parts along dimension 0, may hold values from -6 to 6
- gate_input: bfloat16 [64, 4, 4096], P(('groups', 'replica')), parts along dimension 0, may hold values from -6 to 6
- decay_rate: float32 [32], replicated, may hold values from 0.05 to 1.5
- norm_gain: float32 [4096], replicated, may hold values from 0.1 to 1.9
- out_weight: bfloat16 [4096, 3072], P('replica'), may hold values from -0.09375 to 0.09375
- prompt_states: bfloat16 [8, 4096, 128], P('groups', 'replica'), parts along dimension 0, may hold values from -4 to 4
- group_sizes: int32 [8], P('groups'), parts along dimension 0, may hold values from 1 to 16, 32 in all
Outputs:
- mixed: bfloat16 [64, 4, 3072], P(('groups', 'replica')), parts along dimension 0
The draws below stay inside these ranges and needn't reach their ends.
There are 2 independent parts, one for each index of `groups`. The reference program is written for one: setup_inputs(seed, part) draws one part's arguments, and reference() takes and returns one part's arrays. A program takes and returns all parts, laid end to end along the dimension named above; an argument that names none is the same for every part. Nothing has to cross between parts.
Inputs may be any that keep to these rules, and one draw needn't show every extreme that they name: `group_sizes`: the group sizes sum to 32, and the largest is exactly 16.
All inputs are finite; a program needn't handle non-finite values.
Results may differ from the reference program's by a relative error of at most 0.005.
Values may be sent and summed in bfloat16 or wider, within the bound.
No kernel may reach another device: no remote copies, remote signals or barrier semaphores. Data moves between devices by JAX's collectives and lax.ppermute only.
A program may use at most 64 MiB of HBM per device.

```python
import math
import jax
import jax.numpy as jnp
import numpy as np
from jax import lax

D = 3072
HEADS = 32
HD = 128
STEPS = 4
ROWS = 32
PROMPTS = 4
MOST = 16


def steps_of(rng, shape, cuts, low, top_value):
    level = 1.0
    for axis_at, shards_of in cuts:
        heights = jax.random.uniform(jax.random.fold_in(jax.random.fold_in(rng, 6), axis_at), (shards_of,), jnp.float32, low / len(cuts), top_value / len(cuts))
        level = level * jnp.repeat(jnp.exp(heights), shape[axis_at] // shards_of).reshape((-1,) + (1,) * (len(shape) - 1 - axis_at))
    return level


def split_up(number_of, total, bound, slope):
    weights = [(1 << 20) // math.isqrt(grade ** slope) + 1 for grade in range(2, number_of + 1)]
    spare, holding = total - bound - (number_of - 1), [1] * (number_of - 1)
    while spare > 0:
        free = [i for i in range(number_of - 1) if holding[i] < bound]
        pool, remaining = sum([weights[i] for i in free]), spare
        for i in free:
            extra = min(bound - holding[i], max(1, remaining * weights[i] // pool), spare)
            holding[i] = holding[i] + extra
            spare = spare - extra
    return np.array([bound] + holding)


def ragged(key, number_of, total, reach, slope):
    if number_of == 2:
        one = jax.random.randint(key, (), max(1, total - reach), min(reach, total - 1) + 1)
        return jnp.stack([one, total - one])
    lengths = jnp.asarray(split_up(number_of, total, reach, slope), jnp.int32)
    couples = (number_of - 1) // 2
    donor, taker = lengths[1:1 + 2 * couples:2], lengths[2:2 + 2 * couples:2]
    room = jnp.minimum(donor - 1, reach - taker)
    passed = jax.random.randint(jax.random.fold_in(key, 1), (couples,), 0, 1 << 20) % (room + 1)
    lengths = lengths.at[1:1 + 2 * couples:2].set(donor - passed).at[2:2 + 2 * couples:2].set(taker + passed)
    return lengths[jax.random.permutation(jax.random.fold_in(key, 2), number_of)]


def noise(stream_key, dims, scale, limit, cuts=(), kind=jnp.bfloat16):
    array = jax.random.normal(stream_key, dims, jnp.float32) * scale
    if len(cuts) > 0:
        array = steps_of(stream_key, dims, cuts, -0.22, 0.18) * array
    return jnp.clip(array, min=-limit, max=limit).astype(kind)


def setup_inputs(seed: int = 0, part: int = 0) -> dict:
    arg_keys = jax.random.split(jax.random.key(seed), 10)
    part_splits = jax.random.split(jax.random.fold_in(arg_keys[9], part), 10)
    return {
        "queries": noise(part_splits[0], (ROWS, STEPS, HEADS * HD), 0.3, 4.0, ((0, 16),)),
        "keys": noise(part_splits[1], (ROWS, STEPS, HEADS * HD), 0.3, 4.0, ((0, 16),)),
        "values": noise(part_splits[2], (ROWS, STEPS, HEADS * HD), 1.0, 6.0, ((0, 16),)),
        "gate_input": noise(part_splits[3], (ROWS, STEPS, HEADS * HD), 1.0, 6.0, ((0, 16),)),
        "decay_rate": jnp.clip(jnp.exp(jax.random.uniform(arg_keys[4], (HEADS,), jnp.float32, math.log(0.05), math.log(1.5))), 0.05, 1.5),
        "norm_gain": jnp.clip(1.0 + 0.18 * jax.random.normal(arg_keys[5], (HEADS * HD,), jnp.float32), 0.1, 1.9),
        "out_weight": noise(arg_keys[6], (HEADS * HD, D), (HEADS * HD) ** -0.5, 0.09375, ((0, 16),)),
        "prompt_states": noise(part_splits[7], (PROMPTS, HEADS * HD, HD), 0.3, 4.0, ((1, 16),)),
        "group_sizes": ragged(part_splits[8], PROMPTS, ROWS, MOST, 2).astype(jnp.int32),
    }


def reference(queries, keys, values, gate_input, decay_rate, norm_gain, out_weight, prompt_states, group_sizes):
    rows_total, steps_count, features = queries.shape
    head_size = prompt_states.shape[2]
    head_count = features // head_size
    ends = jnp.cumsum(group_sizes).astype(jnp.int32)
    row_ids = jnp.arange(rows_total, dtype=jnp.int32)
    owners = lax.optimization_barrier(jnp.sum((row_ids[:, None] >= ends[None, :]).astype(jnp.int32), axis=1)).astype(jnp.int32)

    def read_one(pair):
        query_row, prompt_id = pair
        state = lax.dynamic_index_in_dim(prompt_states, prompt_id, 0, keepdims=False)
        state = state.astype(jnp.float32).reshape(head_count, head_size, head_size)
        query_four = query_row.astype(jnp.float32).reshape(steps_count, head_count, head_size)
        return jnp.einsum('thd,hde->the', query_four, state, precision=lax.Precision.HIGHEST)
    prompt_read = lax.map(read_one, (queries, owners))
    q_four = queries.astype(jnp.float32).reshape(rows_total, steps_count, head_count, head_size)
    k_four = keys.astype(jnp.float32).reshape(rows_total, steps_count, head_count, head_size)
    v_four = values.astype(jnp.float32).reshape(rows_total, steps_count, head_count, head_size)
    times = jnp.arange(1, steps_count + 1).astype(jnp.float32)
    lead = jnp.exp(-times[:, None] * decay_rate[None, :])
    gap = times[:, None] - times[None, :]
    weights_mix = jnp.where(gap[None] >= 0.0, jnp.exp(-jnp.maximum(gap, 0.0)[None] * decay_rate[:, None, None]), 0.0)
    scores = jnp.einsum('rthd,rshd->rhts', q_four, k_four, precision=lax.Precision.HIGHEST)
    recent = jnp.einsum('rhts,rshe->rthe', scores * weights_mix[None], v_four, precision=lax.Precision.HIGHEST)
    attention = lead[None, :, :, None] * prompt_read + recent
    attention = attention.reshape(rows_total, steps_count, features)
    mean_square = lax.optimization_barrier(jnp.mean(attention * attention, axis=-1, keepdims=True))
    gate = jax.nn.sigmoid(gate_input.astype(jnp.float32))
    hidden = (attention * lax.rsqrt(mean_square + 1e-06) * norm_gain * gate).astype(jnp.bfloat16)
    mixed = jnp.dot(hidden.reshape(rows_total * steps_count, features), out_weight, preferred_element_type=jnp.float32)
    return mixed.astype(jnp.bfloat16).reshape(rows_total, steps_count, out_weight.shape[1])
```

```python
import functools

import jax
import jax.numpy as jnp
from jax import lax
from jax.experimental import pallas as pl
from jax.experimental.pallas import tpu as pltpu
from jax.sharding import PartitionSpec as P

LANES = 128
EPSILON = 1e-06
CORES = 2


def partial_plan(
    queries, keys, values, gate_input, decay_rate, norm_gain, out_weight, prompt_states, group_sizes
):
    replicas = lax.axis_size("replica")
    rows_local, steps_count, features = queries.shape
    head_size = prompt_states.shape[2]
    head_count = features // head_size
    share = prompt_states.shape[1]
    rows_total = rows_local * replicas
    ends = jnp.cumsum(group_sizes)
    row_ids = jnp.arange(rows_total, dtype=jnp.int32)
    owners = jnp.sum((row_ids[:, None] >= ends[None, :]).astype(jnp.int32), axis=1)
    q_four = queries.reshape(rows_local, steps_count, head_count, head_size)
    k_four = keys.reshape(rows_local, steps_count, head_count, head_size)
    v_four = values.astype(jnp.float32).reshape(rows_local, steps_count, head_count, head_size)
    piece = min(share, head_size)
    pieces_here = share // piece
    per_head = head_size // piece
    query_parts = queries.reshape(rows_local, steps_count, replicas, share)
    held_queries = lax.all_to_all(query_parts, "replica", split_axis=2, concat_axis=0, tiled=True)
    held_queries = held_queries.reshape(rows_total, steps_count, pieces_here, piece)
    held_states = jnp.take(prompt_states, owners, axis=0).reshape(
        rows_total, pieces_here, piece, head_size
    )
    partial_value = jnp.einsum(
        "rtcd,rcde->rtce", held_queries, held_states, preferred_element_type=jnp.float32
    )
    partial_value = partial_value.reshape(replicas, rows_local, steps_count, pieces_here, head_size)
    returned = lax.all_to_all(partial_value, "replica", split_axis=0, concat_axis=0, tiled=True)
    returned = jnp.moveaxis(returned, 0, 2)
    returned = returned.reshape(rows_local, steps_count, head_count, per_head, head_size)
    prompt_read = jnp.sum(returned, axis=3)
    times = jnp.arange(1, steps_count + 1).astype(jnp.float32)
    lead = jnp.exp(-times[:, None] * decay_rate[None, :])
    gap = times[:, None] - times[None, :]
    weights_mix = jnp.where(
        gap[None] >= 0.0, jnp.exp(-jnp.maximum(gap, 0.0)[None] * decay_rate[:, None, None]), 0.0
    )
    scores = jnp.einsum("rthd,rshd->rhts", q_four, k_four, preferred_element_type=jnp.float32)
    recent = jnp.einsum(
        "rhts,rshe->rthe", scores * weights_mix[None], v_four, precision=lax.Precision.HIGHEST
    )
    attention = lead[None, :, :, None] * prompt_read + recent
    attention = attention.reshape(rows_local, steps_count, features)
    mean_square = jnp.mean(attention * attention, axis=-1, keepdims=True)
    gate = jax.nn.sigmoid(gate_input.astype(jnp.float32))
    hidden = (attention * lax.rsqrt(mean_square + EPSILON) * norm_gain * gate).astype(jnp.bfloat16)
    hidden = hidden.reshape(rows_local * steps_count, features)
    columns_held = lax.all_to_all(hidden, "replica", split_axis=1, concat_axis=0, tiled=True)
    mixed = lax.psum_scatter(
        jnp.dot(columns_held, out_weight, preferred_element_type=jnp.float32),
        "replica",
        scatter_dimension=0,
        tiled=True,
    )
    return mixed.astype(jnp.bfloat16).reshape(rows_local, steps_count, out_weight.shape[1])


def pack_kernel(q_ref, k_ref, v_ref, g_ref, send_ref):
    chips, _, _, width = send_ref.shape
    rows, steps, _ = q_ref.shape
    for array, ref in enumerate((q_ref, k_ref, v_ref, g_ref)):
        for chip in range(chips):
            window = slice(chip * width, (chip + 1) * width)
            for row in range(rows):
                send_ref[chip, array, row * steps : (row + 1) * steps, :] = ref[row, :, window]


def head_kernel(
    rows, steps, rate_ref, size_ref, recv_ref, gain_ref, own_state, other_state, own_weight,
    other_weight, part_ref, hidden_ref, weight_ref, sems,
):
    chips, _, per_chip, _ = recv_ref.shape
    count = chips * per_chip
    prompts, share, head = own_state.shape
    heads_here = share // head
    device = lax.axis_index("replica")
    chip = device // CORES
    core = lax.rem(device, CORES)
    copies = [
        pltpu.make_async_copy(source, weight_ref.at[slot * share : (slot + 1) * share], sems.at[slot])
        for slot, source in enumerate((own_weight, other_weight))
    ]
    for copy in copies:
        copy.start()
    index = lax.broadcasted_iota(jnp.int32, (count, head), 0)
    row = (index // per_chip * CORES + core) * rows + index % per_chip // steps
    time = (index % steps + 1).astype(jnp.float32)
    here = []
    first = jnp.int32(0)
    for prompt in range(prompts):
        last = first + size_ref[prompt]
        here.append((row >= first) & (row < last))
        first = last
    left = lax.broadcasted_iota(jnp.int32, (count, count), 0)
    right = lax.broadcasted_iota(jnp.int32, (count, count), 1)
    joined = (left // steps == right // steps) & (left >= right)
    gap = jnp.maximum(left - right, 0).astype(jnp.float32)
    squares = jnp.zeros((count, head), jnp.float32)
    for slot, state in enumerate((own_state, other_state)):
        place = core if slot == 0 else CORES - 1 - core
        for part in range(heads_here):
            number = (chip * CORES + place) * heads_here + part
            rate = rate_ref[number]
            window = pl.ds(pl.multiple_of(place * share + part * head, head), head)
            query, key, value, gate = (
                recv_ref[:, array, :, window].astype(jnp.float32).reshape(count, head)
                for array in range(4)
            )
            held = slice(part * head, (part + 1) * head)
            read = jnp.zeros((count, head), jnp.float32)
            for prompt in range(prompts):
                picked = jnp.where(here[prompt], query, 0.0).astype(jnp.bfloat16)
                read += jnp.dot(picked, state[prompt, held, :], preferred_element_type=jnp.float32)
            scores = lax.dot_general(
                query.astype(jnp.bfloat16),
                key.astype(jnp.bfloat16),
                (((1,), (1,)), ((), ())),
                preferred_element_type=jnp.float32,
            )
            scores = jnp.where(joined, scores * jnp.exp(-gap * rate), 0.0)
            high = scores.astype(jnp.bfloat16)
            rest = scores - high.astype(jnp.float32)
            low = rest.astype(jnp.bfloat16)
            value = value.astype(jnp.bfloat16)
            recent = jnp.dot(high, value, preferred_element_type=jnp.float32)
            recent += jnp.dot(low, value, preferred_element_type=jnp.float32)
            attention = jnp.exp(-time * rate) * read + recent
            squares += attention * attention
            scaled = attention * gain_ref[pl.ds(number, 1), :] * jax.nn.sigmoid(gate)
            column = slot * share + part * head
            hidden_ref[:, column : column + head] = scaled.astype(jnp.bfloat16)
    total = jnp.sum(squares, axis=1, keepdims=True)
    high = total.astype(jnp.bfloat16).astype(jnp.float32)
    middle = (total - high).astype(jnp.bfloat16).astype(jnp.float32)
    low = total - high - middle
    lane = lax.broadcasted_iota(jnp.int32, (count, LANES), 1)
    tail = jnp.where(lane == 0, high, jnp.where(lane == 1, middle, jnp.where(lane == 2, low, 0.0)))
    width = own_weight.shape[1]
    part_ref[:, :, width:] = tail.reshape(chips, per_chip, LANES).astype(part_ref.dtype)
    for copy in copies:
        copy.wait()
    tile = 512 if width % 512 == 0 else LANES
    for start in range(0, width, tile):
        columns = slice(start, start + tile)
        block = jnp.dot(hidden_ref[...], weight_ref[:, columns], preferred_element_type=jnp.float32)
        part_ref[:, :, columns] = block.reshape(chips, per_chip, tile).astype(part_ref.dtype)


def finish_kernel(features, part_ref, mixed_ref):
    rows, steps, width = mixed_ref.shape
    tail = jnp.sum(part_ref[:, :, width:].astype(jnp.float32), axis=0)
    squares = jnp.sum(tail, axis=1, keepdims=True)
    scale = lax.rsqrt(squares / features + EPSILON)
    tile = 512 if width % 512 == 0 else LANES
    for start in range(0, width, tile):
        columns = slice(start, start + tile)
        block = jnp.sum(part_ref[:, :, columns].astype(jnp.float32), axis=0) * scale
        mixed_ref[:, :, columns] = block.reshape(rows, steps, tile).astype(mixed_ref.dtype)


def whole_plan(
    queries, keys, values, gate_input, decay_rate, norm_gain, out_weight, prompt_states, group_sizes
):
    replicas = lax.axis_size("replica")
    rows, steps, features = queries.shape
    prompts, share, head = prompt_states.shape
    width = out_weight.shape[1]
    chips = replicas // CORES
    per_chip = rows * steps
    wide = share * CORES
    swap = [(i, i + 1 - 2 * (i % CORES)) for i in range(replicas)]
    peers = [[i * CORES + core for i in range(chips)] for core in range(CORES)]
    other_state = lax.ppermute(prompt_states, "replica", swap)
    other_weight = lax.ppermute(out_weight, "replica", swap)
    vmem = pl.BlockSpec(memory_space=pltpu.VMEM)
    smem = pl.BlockSpec(memory_space=pltpu.SMEM)
    whole = pl.BlockSpec(memory_space=pl.ANY)
    limit = pltpu.CompilerParams(vmem_limit_bytes=24 << 20)
    sent = pl.pallas_call(
        pack_kernel,
        out_shape=jax.ShapeDtypeStruct((chips, 4, per_chip, wide), queries.dtype),
        in_specs=[vmem] * 4,
        out_specs=vmem,
        compiler_params=limit,
        name="pack",
    )(queries, keys, values, gate_input)
    exchange = functools.partial(
        lax.all_to_all,
        axis_name="replica",
        split_axis=0,
        concat_axis=0,
        tiled=True,
        axis_index_groups=peers,
    )
    held = exchange(sent)
    parts = pl.pallas_call(
        functools.partial(head_kernel, rows, steps),
        out_shape=jax.ShapeDtypeStruct((chips, per_chip, width + LANES), jnp.bfloat16),
        in_specs=[smem, smem, vmem, vmem, vmem, vmem, whole, whole],
        out_specs=vmem,
        scratch_shapes=[
            pltpu.VMEM((chips * per_chip, wide), jnp.bfloat16),
            pltpu.VMEM((wide, width), out_weight.dtype),
            pltpu.SemaphoreType.DMA((2,)),
        ],
        compiler_params=limit,
        name="heads",
    )(
        decay_rate,
        group_sizes,
        held,
        norm_gain.reshape(features // head, head),
        prompt_states,
        other_state,
        out_weight,
        other_weight,
    )
    returned = exchange(parts)
    return pl.pallas_call(
        functools.partial(finish_kernel, features),
        out_shape=jax.ShapeDtypeStruct((rows, steps, width), jnp.bfloat16),
        in_specs=[vmem],
        out_specs=vmem,
        compiler_params=limit,
        name="finish",
    )(returned)


def on_device(*arguments):
    states = arguments[7]
    replicas = lax.axis_size("replica")
    if states.shape[1] % states.shape[2] == 0 and replicas % CORES == 0:
        return whole_plan(*arguments)
    return partial_plan(*arguments)


def solution(mesh):
    in_specs = (
        P(("groups", "replica"), None, None),
        P(("groups", "replica"), None, None),
        P(("groups", "replica"), None, None),
        P(("groups", "replica"), None, None),
        P(),
        P(),
        P("replica", None),
        P("groups", "replica", None),
        P("groups"),
    )
    out_specs = P(("groups", "replica"), None, None)
    return jax.shard_map(
        on_device, mesh=mesh, in_specs=in_specs, out_specs=out_specs, check_vma=False
    )
```

```python
import functools

import jax
import jax.numpy as jnp
from jax import lax
from jax.experimental import pallas as pl
from jax.experimental.pallas import tpu as pltpu
from jax.sharding import PartitionSpec as P


LANES = 128
EPSILON = 1e-06
CORES = 2


def partial_plan(
    queries, keys, values, gate_input, decay_rate, norm_gain, out_weight, prompt_states, group_sizes
):
    replicas = lax.axis_size("replica")
    rows_local, steps_count, features = queries.shape
    head_size = prompt_states.shape[2]
    head_count = features // head_size
    share = prompt_states.shape[1]
    rows_total = rows_local * replicas
    ends = jnp.cumsum(group_sizes)
    row_ids = jnp.arange(rows_total, dtype=jnp.int32)
    owners = jnp.sum((row_ids[:, None] >= ends[None, :]).astype(jnp.int32), axis=1)
    q_four = queries.reshape(rows_local, steps_count, head_count, head_size)
    k_four = keys.reshape(rows_local, steps_count, head_count, head_size)
    v_four = values.astype(jnp.float32).reshape(rows_local, steps_count, head_count, head_size)
    piece = min(share, head_size)
    pieces_here = share // piece
    per_head = head_size // piece
    query_parts = queries.reshape(rows_local, steps_count, replicas, share)
    held_queries = lax.all_to_all(query_parts, "replica", split_axis=2, concat_axis=0, tiled=True)
    held_queries = held_queries.reshape(rows_total, steps_count, pieces_here, piece)
    held_states = jnp.take(prompt_states, owners, axis=0).reshape(
        rows_total, pieces_here, piece, head_size
    )
    partial_value = jnp.einsum(
        "rtcd,rcde->rtce", held_queries, held_states, preferred_element_type=jnp.float32
    )
    partial_value = partial_value.reshape(replicas, rows_local, steps_count, pieces_here, head_size)
    returned = lax.all_to_all(partial_value, "replica", split_axis=0, concat_axis=0, tiled=True)
    returned = jnp.moveaxis(returned, 0, 2)
    returned = returned.reshape(rows_local, steps_count, head_count, per_head, head_size)
    prompt_read = jnp.sum(returned, axis=3)
    times = jnp.arange(1, steps_count + 1).astype(jnp.float32)
    lead = jnp.exp(-times[:, None] * decay_rate[None, :])
    gap = times[:, None] - times[None, :]
    weights_mix = jnp.where(
        gap[None] >= 0.0, jnp.exp(-jnp.maximum(gap, 0.0)[None] * decay_rate[:, None, None]), 0.0
    )
    scores = jnp.einsum("rthd,rshd->rhts", q_four, k_four, preferred_element_type=jnp.float32)
    recent = jnp.einsum(
        "rhts,rshe->rthe", scores * weights_mix[None], v_four, precision=lax.Precision.HIGHEST
    )
    attention = lead[None, :, :, None] * prompt_read + recent
    attention = attention.reshape(rows_local, steps_count, features)
    mean_square = jnp.mean(attention * attention, axis=-1, keepdims=True)
    gate = jax.nn.sigmoid(gate_input.astype(jnp.float32))
    hidden = (attention * lax.rsqrt(mean_square + EPSILON) * norm_gain * gate).astype(jnp.bfloat16)
    hidden = hidden.reshape(rows_local * steps_count, features)
    columns_held = lax.all_to_all(hidden, "replica", split_axis=1, concat_axis=0, tiled=True)
    mixed = lax.psum_scatter(
        jnp.dot(columns_held, out_weight, preferred_element_type=jnp.float32),
        "replica",
        scatter_dimension=0,
        tiled=True,
    )
    return mixed.astype(jnp.bfloat16).reshape(rows_local, steps_count, out_weight.shape[1])


def pack_kernel(q_hbm, k_hbm, v_hbm, g_hbm, send_ref, held_ref, sems):
    chips, _, _, width = send_ref.shape
    _, rows, steps, _ = held_ref.shape
    copies = [
        pltpu.make_async_copy(source, held_ref.at[array], sems.at[array])
        for array, source in enumerate((q_hbm, k_hbm, v_hbm, g_hbm))
    ]
    for copy in copies:
        copy.start()
    for array, copy in enumerate(copies):
        copy.wait()
        for chip in range(chips):
            window = slice(chip * width, (chip + 1) * width)
            for row in range(rows):
                send_ref[chip, array, row * steps : (row + 1) * steps, :] = held_ref[
                    array, row, :, window
                ]


def prepare_kernel(
    rows, steps, heads_here, rate_hbm, size_hbm, _, gain_hbm, state_hbm, state_ref, gain_ref, mix_ref,
    lead_ref, owner_ref, rate_ref, size_ref, sems,
):
    heads, count, _ = mix_ref.shape
    head = lead_ref.shape[2]
    prompts = size_hbm.shape[0]
    device = lax.axis_index("replica")
    chip = device // CORES
    core = lax.rem(device, CORES)
    copies = [
        pltpu.make_async_copy(source, target, sems.at[number])
        for number, (source, target) in enumerate(
            (
                (rate_hbm, rate_ref),
                (size_hbm, size_ref),
                (state_hbm, state_ref),
                (gain_hbm, gain_ref),
            )
        )
    ]
    for copy in copies:
        copy.start()
    left = lax.broadcasted_iota(jnp.int32, (count, count), 0)
    right = lax.broadcasted_iota(jnp.int32, (count, count), 1)
    joined = (left // steps == right // steps) & (left >= right)
    gap = jnp.maximum(left - right, 0).astype(jnp.float32)
    index = lax.broadcasted_iota(jnp.int32, (count, head), 0)
    time = (index % steps + 1).astype(jnp.float32)
    per_chip = rows * steps
    row = (index // per_chip * CORES + core) * rows + index % per_chip // steps
    for copy in copies:
        copy.wait()
    owner = jnp.zeros((count, head), jnp.int32)
    end = jnp.int32(0)
    for prompt in range(prompts):
        end = end + size_ref[prompt]
        owner += (row >= end).astype(jnp.int32)
    owner_ref[...] = owner
    for number in range(heads):
        slot, part = divmod(number, heads_here)
        place = core if slot == 0 else CORES - 1 - core
        rate = rate_ref[(chip * CORES + place) * heads_here + part]
        mix_ref[number] = jnp.where(joined, jnp.exp(-gap * rate), 0.0)
        lead_ref[number] = jnp.exp(-time * rate)


def head_kernel(
    recv_ref, gain_ref, mix_ref, lead_ref, owner_ref, own_state, other_state, own_hbm, other_weight,
    part_ref, hidden_ref, own_weight, sem,
):
    chips, _, per_chip, _ = recv_ref.shape
    count = chips * per_chip
    prompts, share, head = own_state.shape
    heads_here = share // head
    device = lax.axis_index("replica")
    chip = device // CORES
    core = lax.rem(device, CORES)
    fetch = pltpu.make_async_copy(own_hbm, own_weight, sem)
    fetch.start()
    owner = owner_ref[...]
    here = [owner == prompt for prompt in range(prompts)]
    squares = jnp.zeros((count, head), jnp.float32)
    for slot, state in enumerate((own_state, other_state)):
        place = core if slot == 0 else CORES - 1 - core
        for part in range(heads_here):
            number = (chip * CORES + place) * heads_here + part
            window = pl.ds(pl.multiple_of(place * share + part * head, head), head)
            query, key, value, gate = (
                recv_ref[:, array, :, window].astype(jnp.float32).reshape(count, head)
                for array in range(4)
            )
            held = slice(part * head, (part + 1) * head)
            read = jnp.zeros((count, head), jnp.float32)
            for prompt in range(prompts):
                picked = jnp.where(here[prompt], query, 0.0).astype(jnp.bfloat16)
                read += jnp.dot(picked, state[prompt, held, :], preferred_element_type=jnp.float32)
            scores = lax.dot_general(
                query.astype(jnp.bfloat16),
                key.astype(jnp.bfloat16),
                (((1,), (1,)), ((), ())),
                preferred_element_type=jnp.float32,
            )
            scores = scores * mix_ref[slot * heads_here + part]
            high = scores.astype(jnp.bfloat16)
            rest = scores - high.astype(jnp.float32)
            low = rest.astype(jnp.bfloat16)
            value = value.astype(jnp.bfloat16)
            recent = jnp.dot(high, value, preferred_element_type=jnp.float32)
            recent += jnp.dot(low, value, preferred_element_type=jnp.float32)
            attention = lead_ref[slot * heads_here + part] * read + recent
            squares += attention * attention
            scaled = attention * gain_ref[pl.ds(number, 1), :] * jax.nn.sigmoid(gate)
            column = slot * share + part * head
            hidden_ref[:, column : column + head] = scaled.astype(jnp.bfloat16)
    total = jnp.sum(squares, axis=1, keepdims=True)
    high = total.astype(jnp.bfloat16).astype(jnp.float32)
    middle = (total - high).astype(jnp.bfloat16).astype(jnp.float32)
    low = total - high - middle
    lane = lax.broadcasted_iota(jnp.int32, (count, LANES), 1)
    tail = jnp.where(lane == 0, high, jnp.where(lane == 1, middle, jnp.where(lane == 2, low, 0.0)))
    width = own_weight.shape[1]
    part_ref[:, :, width:] = tail.reshape(chips, per_chip, LANES).astype(part_ref.dtype)
    fetch.wait()
    tile = 512 if width % 512 == 0 else LANES
    for start in range(0, width, tile):
        columns = slice(start, start + tile)
        block = jnp.dot(
            hidden_ref[:, :share], own_weight[:, columns], preferred_element_type=jnp.float32
        )
        block += jnp.dot(
            hidden_ref[:, share:], other_weight[:, columns], preferred_element_type=jnp.float32
        )
        part_ref[:, :, columns] = block.reshape(chips, per_chip, tile).astype(part_ref.dtype)


def finish_kernel(features, part_ref, mixed_ref):
    rows, steps, width = mixed_ref.shape
    tail = jnp.sum(part_ref[:, :, width:].astype(jnp.float32), axis=0)
    squares = jnp.sum(tail, axis=1, keepdims=True)
    scale = lax.rsqrt(squares / features + EPSILON)
    tile = 512 if width % 512 == 0 else LANES
    for start in range(0, width, tile):
        columns = slice(start, start + tile)
        block = jnp.sum(part_ref[:, :, columns].astype(jnp.float32), axis=0) * scale
        mixed_ref[:, :, columns] = block.reshape(rows, steps, tile).astype(mixed_ref.dtype)


def whole_plan(
    queries, keys, values, gate_input, decay_rate, norm_gain, out_weight, prompt_states, group_sizes
):
    replicas = lax.axis_size("replica")
    rows, steps, features = queries.shape
    _, share, head = prompt_states.shape
    width = out_weight.shape[1]
    chips = replicas // CORES
    per_chip = rows * steps
    wide = share * CORES
    swap = [(i, i + 1 - 2 * (i % CORES)) for i in range(replicas)]
    peers = [[i * CORES + core for i in range(chips)] for core in range(CORES)]
    queries, keys, values, gate_input, decay_rate, group_sizes, gains, near_state, near_weight = (
        pltpu.with_memory_space_constraint(array, pltpu.HBM)
        for array in (
            queries,
            keys,
            values,
            gate_input,
            decay_rate,
            group_sizes,
            norm_gain.reshape(features // head, head),
            prompt_states,
            out_weight,
        )
    )
    vmem = pl.BlockSpec(memory_space=pltpu.VMEM)
    smem = pl.BlockSpec(memory_space=pltpu.SMEM)
    far = pl.BlockSpec(memory_space=pltpu.HBM)
    limit = pltpu.CompilerParams(vmem_limit_bytes=24 << 20)
    sent = pl.pallas_call(
        pack_kernel,
        out_shape=jax.ShapeDtypeStruct((chips, 4, per_chip, wide), queries.dtype),
        in_specs=[far] * 4,
        out_specs=vmem,
        scratch_shapes=[
            pltpu.VMEM((4, rows, steps, features), queries.dtype),
            pltpu.SemaphoreType.DMA((4,)),
        ],
        compiler_params=limit,
        name="pack",
    )(queries, keys, values, gate_input)
    exchange = functools.partial(
        lax.all_to_all,
        axis_name="replica",
        split_axis=0,
        concat_axis=0,
        tiled=True,
        axis_index_groups=peers,
    )
    held = exchange(sent)
    other_state = lax.ppermute(prompt_states, "replica", swap)
    other_weight = lax.ppermute(out_weight, "replica", swap)
    count = chips * per_chip
    heads = wide // head
    state, gain, mix, lead, owner = pl.pallas_call(
        functools.partial(prepare_kernel, rows, steps, share // head),
        out_shape=(
            jax.ShapeDtypeStruct(prompt_states.shape, prompt_states.dtype),
            jax.ShapeDtypeStruct((features // head, head), jnp.float32),
            jax.ShapeDtypeStruct((heads, count, count), jnp.float32),
            jax.ShapeDtypeStruct((heads, count, head), jnp.float32),
            jax.ShapeDtypeStruct((count, head), jnp.int32),
        ),
        in_specs=[far] * 5,
        out_specs=(vmem,) * 5,
        scratch_shapes=[
            pltpu.SMEM(decay_rate.shape, decay_rate.dtype),
            pltpu.SMEM(group_sizes.shape, group_sizes.dtype),
            pltpu.SemaphoreType.DMA((4,)),
        ],
        compiler_params=limit,
        name="prepare",
    )(decay_rate, group_sizes, sent, gains, near_state)
    parts = pl.pallas_call(
        head_kernel,
        out_shape=jax.ShapeDtypeStruct((chips, per_chip, width + LANES), jnp.bfloat16),
        in_specs=[vmem] * 7 + [far, vmem],
        out_specs=vmem,
        scratch_shapes=[
            pltpu.VMEM((count, wide), jnp.bfloat16),
            pltpu.VMEM(out_weight.shape, out_weight.dtype),
            pltpu.SemaphoreType.DMA(()),
        ],
        compiler_params=limit,
        name="heads",
    )(held, gain, mix, lead, owner, state, other_state, near_weight, other_weight)
    returned = exchange(parts)
    return pl.pallas_call(
        functools.partial(finish_kernel, features),
        out_shape=jax.ShapeDtypeStruct((rows, steps, width), jnp.bfloat16),
        in_specs=[vmem],
        out_specs=vmem,
        compiler_params=limit,
        name="finish",
    )(returned)


def on_device(*arguments):
    states = arguments[7]
    replicas = lax.axis_size("replica")
    if states.shape[1] % states.shape[2] == 0 and replicas % CORES == 0:
        return whole_plan(*arguments)
    return partial_plan(*arguments)


def solution(mesh):
    in_specs = (
        P(("groups", "replica"), None, None),
        P(("groups", "replica"), None, None),
        P(("groups", "replica"), None, None),
        P(("groups", "replica"), None, None),
        P(),
        P(),
        P("replica", None),
        P("groups", "replica", None),
        P("groups"),
    )
    out_specs = P(("groups", "replica"), None, None)
    return jax.shard_map(
        on_device, mesh=mesh, in_specs=in_specs, out_specs=out_specs, check_vma=False
    )
```
